32 devices in a mesh: row: 4 (over y, core), col: 8 (over z, x).
Axes of the slice: x: 2, y: 2, z: 4, core: 2. Of those that a mesh axis runs over, the one named last changes fastest.
Arguments:
- tokens: bfloat16 [3072, 6144], P('row'), may hold values from -6 to 6
- routes: int32 [3072, 2], P('row'), may hold values from 0 to 7, as said below
- w_master: float32 [6144, 2, 9216], P('row', None, 'col'), may hold values from -1 to 1
- d_hidden: bfloat16 [768, 9216], P('row', 'col'), may hold values from -6 to 6
Outputs:
- hidden: bfloat16 [768, 9216], P('row', 'col')
- update: float32 [6144, 2, 9216], P('row', None, 'col')
- new_master: float32 [6144, 2, 9216], P('row', None, 'col')
The draws below stay inside these ranges and needn't reach their ends.
Inputs may be any that keep to these rules, and one draw needn't show every extreme that they name: `routes`: in every aligned block of 768 tokens exactly 192 tokens name expert 0; the two experts of a token differ; every expert is named.
All inputs are finite; a program needn't handle non-finite values. Where the reference program divides by a largest or mean magnitude, that divisor is 1e-20 or more.
Results may differ from the reference program's by a relative error of at most 0.023.
Values may be sent and summed in bfloat16 or wider, within the bound.
A program may use at most 128 MiB of HBM per device.

```python
import jax
import jax.numpy as jnp
from jax import lax

D = 6144
EXPERTS = 8
FFW = 9216
BLK = 128
TOK_ROW = 768
CAP = 192
TOKENS = 3072
SLOTS = 768
N_ROW = 4


def draw_routes(key, part):
    blocks = TOKENS // TOK_ROW
    keys = jax.random.split(jax.random.fold_in(key, 11), 4)
    orders = jax.vmap(lambda k: jax.random.permutation(k, TOK_ROW))(jax.random.split(keys[0], blocks))
    chosen = orders < CAP
    first = jax.random.randint(keys[1], (blocks, TOK_ROW), 1, EXPERTS)
    offset = jax.random.randint(keys[2], (blocks, TOK_ROW), 1, EXPERTS - 1)
    second = (first - 1 + offset) % (EXPERTS - 1) + 1
    flipped = jax.random.randint(keys[3], (blocks, TOK_ROW), 0, 2)
    leading = jnp.where(chosen, 0, first)
    column_one = jnp.where(flipped == 1, second, leading)
    column_two = jnp.where(flipped == 1, leading, second)
    return jnp.stack([column_one, column_two], axis=-1).reshape(TOKENS, 2).astype(jnp.int32)


def draw_w_master(key, part):
    keys = jax.random.split(jax.random.fold_in(key, 23), 3)
    row_bands = jnp.exp(jax.random.uniform(keys[0], (D // BLK,), jnp.float32, 0.0, jnp.log(10.0)))
    row_scale = jnp.repeat(row_bands, BLK)
    col_bands = jnp.exp(jax.random.uniform(keys[1], (2, FFW // 32), jnp.float32, jnp.log(0.3), jnp.log(3.0)))
    col_scale = jnp.repeat(col_bands, 32, axis=1)
    base = jnp.clip(jax.random.normal(keys[2], (D, 2, FFW), jnp.float32), -6.0, 6.0)
    values = base * row_scale[:, None, None] * col_scale[None, :, :] / jnp.sqrt(21.5 * D)
    return values.astype(jnp.float32)


def block_scale(rng, shape, cuts, least, high):
    loudness, own = 1.0, jax.random.fold_in(rng, 6)
    for dim, parts in cuts:
        draws = jnp.exp(jax.random.uniform(jax.random.fold_in(own, dim), (parts,), jnp.float32, least / len(cuts), high / len(cuts)))
        loudness = loudness * jnp.repeat(draws, shape[dim] // parts).reshape([-1 if axis == dim else 1 for axis in range(len(shape))])
    return loudness


def gaussian(key, shape, deviation, most, pieces=(), held_as=jnp.bfloat16):
    drawn = deviation * jax.random.normal(key, shape, jnp.float32)
    if pieces:
        drawn = drawn * block_scale(key, shape, pieces, -0.22, 0.18)
    return jnp.clip(drawn, -most, most).astype(held_as)


def setup_inputs(seed: int = 0) -> dict:
    streams_of = jax.random.split(jax.random.key(seed), 5)
    tokens = gaussian(streams_of[0], (TOKENS, D), 1.0, 6.0, ((0, 4),))
    routes = draw_routes(jax.random.fold_in(streams_of[4], 71), 0)
    w_master = draw_w_master(jax.random.fold_in(streams_of[4], 71), 0)
    d_hidden = gaussian(streams_of[3], (SLOTS, FFW), 1.0, 6.0, ((0, 4), (1, 8)))
    return {"tokens": tokens, "routes": routes, "w_master": w_master, "d_hidden": d_hidden}


epsilon = 1e-6
quant_range = 448.0
learn_rate = 0.05


def reference(tokens, routes, w_master, d_hidden):
    colmax = jnp.max(jnp.abs(w_master), axis=0)
    wscale = (colmax + epsilon) / quant_range
    quantized = (w_master / wscale).astype(jnp.bfloat16)
    routed = jnp.any(routes == 0, axis=1).reshape(N_ROW, TOK_ROW)

    def choose(flags):
        return jnp.nonzero(flags, size=CAP)[0].astype(jnp.int32)

    positions = jax.vmap(choose)(routed) + (jnp.arange(N_ROW, dtype=jnp.int32) * TOK_ROW)[:, None]
    slot_rows = tokens[positions.reshape(-1)]
    group_width = D // N_ROW
    weight_groups = quantized.reshape(N_ROW, group_width, 2 * FFW)
    row_slices = jnp.transpose(slot_rows.reshape(SLOTS, N_ROW, group_width), (1, 0, 2))

    def add_rows(carry_sum, items):
        slot_part, weight_part = items
        term = jnp.dot(slot_part, weight_part, preferred_element_type=jnp.float32)
        rounded = lax.optimization_barrier(term.astype(jnp.bfloat16)).astype(jnp.float32)
        return carry_sum + rounded, None

    summed, _ = lax.scan(add_rows, jnp.zeros((SLOTS, 2 * FFW), jnp.float32), (row_slices, weight_groups))
    projected = summed.reshape(SLOTS, 2, FFW) * wscale
    gate_pre = projected[:, 0]
    up_pre = projected[:, 1]
    gate_sig = jax.nn.sigmoid(gate_pre)
    gate_act = gate_pre * gate_sig
    hidden = (gate_act * up_pre).astype(jnp.bfloat16)
    upstream = d_hidden.astype(jnp.float32)
    grad_gate = upstream * up_pre * gate_sig * (1.0 + gate_pre * (1.0 - gate_sig))
    grad_up = upstream * gate_act
    grad_pre = jnp.stack([grad_gate, grad_up], axis=1).astype(jnp.bfloat16).reshape(N_ROW, CAP, 2 * FFW)
    group_rows = slot_rows.reshape(N_ROW, CAP, D)

    def add_group(carry_sum, items):
        rows_part, grads_part = items
        block_term = lax.dot_general(rows_part, grads_part, (((0,), (0,)), ((), ())), preferred_element_type=jnp.float32)
        rounded = lax.optimization_barrier(block_term.astype(jnp.bfloat16)).astype(jnp.float32)
        return carry_sum + rounded, None

    grad_full, _ = lax.scan(add_group, jnp.zeros((D, 2 * FFW), jnp.float32), (group_rows, grad_pre))
    grad_full = grad_full.reshape(D // BLK, BLK, 2, FFW)
    block_max = jnp.max(jnp.abs(grad_full), axis=(1, 3))
    update = (grad_full / (block_max[:, None, :, None] + epsilon)).reshape(D, 2, FFW)
    new_master = w_master - learn_rate * colmax * update
    return hidden, update, new_master
```

```python
import jax
import jax.numpy as jnp
from jax import lax
from jax.experimental import pallas as pl
from jax.experimental.pallas import tpu as pltpu
from jax.sharding import PartitionSpec as P

BLK = 128


epsilon = 1e-06
quant_range = 448.0
learn_rate = 0.05


def on_device_plain(tokens, routes, w_master, d_hidden):
    rows_local, _, columns = w_master.shape
    slots = d_hidden.shape[0]
    colmax = lax.pmax(jnp.max(jnp.abs(w_master), axis=0), "row")
    wscale = (colmax + epsilon) / quant_range
    quantized = (w_master / wscale).astype(jnp.bfloat16).reshape(rows_local, 2 * columns)
    flat_scale = wscale.reshape(2 * columns)
    routed = jnp.any(routes == 0, axis=1)
    picked = jnp.nonzero(routed, size=slots)[0].astype(jnp.int32)
    slot_rows = tokens[picked]
    slot_cols = lax.all_to_all(slot_rows, "row", split_axis=1, concat_axis=0, tiled=True)
    slot_part = lax.slice_in_dim(slot_cols, 0, lax.axis_size("row") * slots, axis=0)
    summed = lax.psum_scatter(
        jnp.dot(slot_part, quantized, preferred_element_type=jnp.float32).astype(jnp.bfloat16),
        "row",
        scatter_dimension=0,
        tiled=True,
    ).astype(jnp.float32)
    projected = (summed * flat_scale).reshape(slots, 2, columns)
    gate_pre = projected[:, 0]
    up_pre = projected[:, 1]
    gate_sig = jax.nn.sigmoid(gate_pre)
    gate_act = gate_pre * gate_sig
    hidden = (gate_act * up_pre).astype(jnp.bfloat16)
    upstream = d_hidden.astype(jnp.float32)
    grad_gate = upstream * up_pre * gate_sig * (1.0 + gate_pre * (1.0 - gate_sig))
    grad_up = upstream * gate_act
    grad_pre = (
        jnp.stack([grad_gate, grad_up], axis=1).astype(jnp.bfloat16).reshape(slots, 2 * columns)
    )
    shard_piece = lax.all_gather(grad_pre, "row", axis=0, tiled=True)
    groups = shard_piece.shape[0] // slots
    slot_part = lax.slice_in_dim(slot_cols, 0, shard_piece.shape[0], axis=0).reshape(
        groups, slots, rows_local
    )
    block_terms = jnp.einsum(
        "gsd,gsf->gdf",
        slot_part,
        shard_piece.reshape(groups, slots, 2 * columns),
        preferred_element_type=jnp.float32,
    )
    rounded = lax.optimization_barrier(block_terms.astype(jnp.bfloat16)).astype(jnp.float32)
    grad_full = jnp.sum(rounded, axis=0)
    grad_blocks = grad_full.reshape(rows_local // BLK, BLK, 2, columns)
    block_max = lax.pmax(jnp.max(jnp.abs(grad_blocks), axis=(1, 3)), "col")
    update = (grad_blocks / (block_max[:, None, :, None] + epsilon)).reshape(rows_local, 2, columns)
    new_master = w_master - learn_rate * colmax * update
    return (hidden, update, new_master)


LANE = 128
SUB = 8


def moved(src, dst, send, recv, to):
    return pltpu.make_async_remote_copy(
        src_ref=src,
        dst_ref=dst,
        send_sem=send,
        recv_sem=recv,
        device_id={"row": to},
        device_id_type=pl.DeviceIdType.MESH,
    )


def forward_kernel(
    mask_ref, dh_ref, tok_hbm, w_hbm, hid_ref, sc_ref, ga_ref, cm_ref,
    tokv, asend, wv, folded, cmx, psend, prec, keep, own, xsend, xrec,
    tok_sem, w_sem, a_send, a_recv, c_send, c_recv, p_send, p_recv,
    x_send, x_recv, ga_send, ga_recv, gp_send, gp_recv, gf_send, gf_recv,
):
    me = lax.axis_index("row")
    core = lax.rem(me, 2)
    partner = me + 1 - 2 * core
    across = lax.rem(me + 2, 4)
    diag = lax.rem(partner + 2, 4)
    where_to = (me, across, partner, diag)
    tiles = ga_ref.shape[0]
    slots = hid_ref.shape[0]
    rows = sc_ref.shape[1]
    toks = mask_ref.shape[1]
    chunks = w_sem.shape[1]
    piece = rows // chunks

    order = (3, 1, 2, 0)
    tok_copies = {}
    for j in order:
        cols = pl.ds(pl.multiple_of(where_to[j] * rows, LANE), rows)
        tok_copies[j] = pltpu.make_async_copy(tok_hbm.at[:, cols], tokv.at[j], tok_sem.at[j])
        tok_copies[j].start()
    w_copies = []
    for k in range(chunks):
        part = pl.ds(k * piece, piece)
        for p in range(2):
            w_copies.append(
                pltpu.make_async_copy(w_hbm.at[part, p, :], wv.at[p, part], w_sem.at[p, k])
            )
            w_copies[-1].start()

    barrier = pltpu.get_barrier_semaphore()
    for j in (1, 2, 3):
        pl.semaphore_signal(
            barrier, inc=1, device_id={"row": where_to[j]}, device_id_type=pl.DeviceIdType.MESH
        )

    mask = mask_ref[...]
    before = lax.broadcasted_iota(jnp.int32, (toks, toks), 0)
    after = lax.broadcasted_iota(jnp.int32, (toks, toks), 1)
    ladder = jnp.where(before < after, 1.0, 0.0).astype(jnp.bfloat16)
    place = jnp.dot(mask, ladder, preferred_element_type=jnp.float32)[0:1, :].astype(jnp.int32)
    flag = mask[0:1, :].astype(jnp.float32)
    slot_id = lax.broadcasted_iota(jnp.int32, (slots, toks), 0)
    pick = jnp.where(slot_id == place, flag, 0.0).astype(jnp.bfloat16)
    pl.semaphore_wait(barrier, 3)

    a_copies = {}
    for j in order:
        tok_copies[j].wait()
        got = jnp.dot(pick, tokv[j], preferred_element_type=jnp.float32).astype(jnp.bfloat16)
        if j == 0:
            sc_ref[0:slots, :] = got
        else:
            asend[j - 1] = got
            a_copies[j] = moved(
                asend.at[j - 1],
                sc_ref.at[pl.ds(j * slots, slots)],
                a_send.at[j - 1],
                a_recv.at[j - 1],
                where_to[j],
            )
            a_copies[j].start()

    folded[...] = jnp.zeros(folded.shape, jnp.float32)
    for k in range(chunks):
        for p in range(2):
            w_copies[2 * k + p].wait()

        def fold(t, carry, k=k):
            cols = pl.ds(pl.multiple_of(t * LANE, LANE), LANE)
            for p in range(2):
                tile = jnp.abs(wv[p, k * piece : (k + 1) * piece, cols])
                best = jnp.max(tile.reshape(-1, SUB, LANE), axis=0)
                folded[p, :, cols] = jnp.maximum(folded[p, :, cols], best)
            return carry

        lax.fori_loop(0, tiles, fold, 0)
    cmx[0] = jnp.zeros(cmx.shape[1:], jnp.float32)
    for p in range(2):
        cmx[0, p : p + 1, :] = jnp.max(folded[p], axis=0, keepdims=True)
    c_copies = []
    for j in (1, 2, 3):
        c_copies.append(moved(cmx.at[0], cmx.at[j], c_send.at[j - 1], c_recv.at[j - 1], where_to[j]))
        c_copies[-1].start()
    for copy in c_copies:
        copy.wait()
    cm_ref[...] = jnp.maximum(jnp.maximum(cmx[0], cmx[1]), jnp.maximum(cmx[2], cmx[3]))
    for j in (3, 1, 2):
        a_copies[j].wait()

    def scale_row(t, p):
        cols = pl.ds(pl.multiple_of(t * LANE, LANE), LANE)
        return (cm_ref[p : p + 1, cols] + epsilon) / quant_range

    def swap(t):
        return moved(psend.at[t], prec.at[t], p_send.at[t], p_recv.at[t], partner)

    def cross(t):
        return moved(xsend.at[t], xrec.at[t], x_send.at[t], x_recv.at[t], across)

    def grad_block(t, j):
        return ga_ref.at[t, pl.ds(j * slots, slots)]

    def share_across(t):
        return moved(grad_block(t, 0), grad_block(t, 1), ga_send.at[t], ga_recv.at[t], across)

    def share_partner(t):
        return moved(grad_block(t, 0), grad_block(t, 2), gp_send.at[t], gp_recv.at[t], partner)

    def forward(t):
        return moved(grad_block(t, 1), grad_block(t, 3), gf_send.at[t], gf_recv.at[t], partner)

    def step(i, carry):
        @pl.when(i < tiles)
        def _():
            t = i
            halves = []
            for p in range(2):
                w = wv[p, :, pl.ds(pl.multiple_of(t * LANE, LANE), LANE)]
                halves.append((w * (1.0 / scale_row(t, p))).astype(jnp.bfloat16))
            quantized = jnp.concatenate(halves, axis=1)
            term = jnp.dot(sc_ref[...], quantized, preferred_element_type=jnp.float32)
            slot = lax.rem(t, 2)
            psend[t] = term[2 * slots :].astype(jnp.bfloat16)
            keep[slot] = term[: 2 * slots]
            swap(t).start()

        @pl.when(jnp.logical_and(i >= 1, i < tiles + 1))
        def _():
            t = i - 1
            slot = lax.rem(t, 2)
            swap(t).wait_recv()
            own[slot] = keep[slot, :slots] + prec[t, :slots].astype(jnp.float32)
            xsend[t] = (keep[slot, slots:] + prec[t, slots:].astype(jnp.float32)).astype(jnp.bfloat16)
            cross(t).start()

        @pl.when(jnp.logical_and(i >= 2, i < tiles + 2))
        def _():
            t = i - 2
            cross(t).wait_recv()
            total = own[lax.rem(t, 2)] + xrec[t].astype(jnp.float32)
            gate_pre = total[:, :LANE] * scale_row(t, 0)
            up_pre = total[:, LANE:] * scale_row(t, 1)
            gate_sig = jax.nn.sigmoid(gate_pre)
            gate_act = gate_pre * gate_sig
            cols = pl.ds(pl.multiple_of(t * LANE, LANE), LANE)
            hid_ref[:, cols] = (gate_act * up_pre).astype(jnp.bfloat16)
            upstream = dh_ref[:, cols].astype(jnp.float32)
            grad_gate = upstream * up_pre * gate_sig * (1.0 + gate_pre * (1.0 - gate_sig))
            grad_up = upstream * gate_act
            ga_ref[t, 0:slots, :] = jnp.concatenate([grad_gate, grad_up], axis=1).astype(jnp.bfloat16)
            share_across(t).start()
            share_partner(t).start()

        @pl.when(i >= 3)
        def _():
            t = i - 3
            share_across(t).wait_recv()
            forward(t).start()

        return carry

    lax.fori_loop(0, tiles + 3, step, 0)

    def finish(t, carry):
        swap(t).wait_send()
        cross(t).wait_send()
        share_across(t).wait_send()
        share_partner(t).wait()
        forward(t).wait()
        return carry

    lax.fori_loop(0, tiles, finish, 0)


def gradient_kernel(sc_ref, ga_ref, grad_ref, top_ref, turned):
    tiles = ga_ref.shape[0]
    depth = grad_ref.shape[0]
    turned[...] = sc_ref[...].T
    blocks = depth // BLK
    tops = tuple(jnp.zeros((SUB, LANE), jnp.float32) for _ in range(2 * blocks))

    def step(t, tops):
        grad = jnp.dot(turned[...], ga_ref[t], preferred_element_type=jnp.float32)
        grad_ref[:, pl.ds(pl.multiple_of(t * 2 * LANE, 2 * LANE), 2 * LANE)] = grad.astype(jnp.bfloat16)
        out = []
        for b in range(blocks):
            for p in range(2):
                tile = jnp.abs(grad[b * BLK : (b + 1) * BLK, p * LANE : (p + 1) * LANE])
                out.append(jnp.maximum(tops[2 * b + p], jnp.max(tile.reshape(-1, SUB, LANE), axis=0)))
        return tuple(out)

    tops = lax.fori_loop(0, tiles, step, tops)
    for n in range(2 * blocks):
        top_ref[0, n] = tops[n]


def update_kernel(inv_ref, cm_ref, w_hbm, grad_hbm, update_hbm, new_hbm, wv, uv, gv, w_sem, g_sem, u_sem, n_sem):
    blocks = g_sem.shape[0]
    columns = wv.shape[2]
    tiles = columns // LANE

    def part(b):
        return pl.ds(pl.multiple_of(b * BLK, BLK), BLK)

    def old(b, p):
        return pltpu.make_async_copy(w_hbm.at[part(b), p, :], wv.at[p, part(b)], w_sem.at[p, b])

    def gradient(b):
        return pltpu.make_async_copy(grad_hbm.at[part(b)], gv.at[part(b)], g_sem.at[b])

    def put_update(b, p):
        return pltpu.make_async_copy(uv.at[p, part(b)], update_hbm.at[part(b), p, :], u_sem.at[p, b])

    def put_new(b, p):
        return pltpu.make_async_copy(wv.at[p, part(b)], new_hbm.at[part(b), p, :], n_sem.at[p, b])

    def begin(b, carry):
        gradient(b).start()
        for p in range(2):
            old(b, p).start()
        return carry

    def step(b, carry):
        gradient(b).wait()
        for p in range(2):
            old(b, p).wait()
            inverse = inv_ref[2 * b + p]
            for t in range(tiles):
                cols = slice(t * LANE, (t + 1) * LANE)
                at = (2 * t + p) * LANE
                update = gv[part(b), at : at + LANE].astype(jnp.float32) * inverse
                uv[p, part(b), cols] = update
                wv[p, part(b), cols] = wv[p, part(b), cols] - (learn_rate * cm_ref[p : p + 1, cols]) * update
            put_update(b, p).start()
            put_new(b, p).start()
        return carry

    def finish(b, carry):
        for p in range(2):
            put_update(b, p).wait()
            put_new(b, p).wait()
        return carry

    lax.fori_loop(0, blocks, begin, 0)
    lax.fori_loop(0, blocks, step, 0)
    lax.fori_loop(0, blocks, finish, 0)


def on_device(tokens, routes, w_master, d_hidden):
    rows, _, columns = w_master.shape
    slots = d_hidden.shape[0]
    toks = tokens.shape[0]
    depth = 3 * BLK
    aligned = columns % LANE == 0 and rows % depth == 0 and slots % 16 == 0 and toks % LANE == 0
    if lax.axis_size("row") != 4 or not aligned:
        return on_device_plain(tokens, routes, w_master, d_hidden)
    tiles = columns // LANE
    bf16, f32 = jnp.bfloat16, jnp.float32
    routed = jnp.any(routes == 0, axis=1).astype(bf16)
    mask = jnp.broadcast_to(routed[None, :], (16, toks))
    chunks = 6
    blocks = rows // BLK
    vmem = pl.BlockSpec(memory_space=pltpu.VMEM)
    hbm = pl.BlockSpec(memory_space=pl.ANY)
    dma = pltpu.SemaphoreType.DMA
    wide = 2 * LANE
    hidden, slot_cols, grads, colmax = pl.pallas_call(
        forward_kernel,
        name="forward_exchange",
        out_shape=(
            jax.ShapeDtypeStruct((slots, columns), bf16),
            jax.ShapeDtypeStruct((4 * slots, rows), bf16),
            jax.ShapeDtypeStruct((tiles, 4 * slots, wide), bf16),
            jax.ShapeDtypeStruct((SUB, columns), f32),
        ),
        in_specs=[vmem, vmem, hbm, hbm],
        out_specs=(vmem, vmem, vmem, vmem),
        scratch_shapes=[
            pltpu.VMEM((4, toks, rows), bf16),
            pltpu.VMEM((3, slots, rows), bf16),
            pltpu.VMEM((2, rows, columns), f32),
            pltpu.VMEM((2, SUB, columns), f32),
            pltpu.VMEM((4, SUB, columns), f32),
            pltpu.VMEM((tiles, 2 * slots, wide), bf16),
            pltpu.VMEM((tiles, 2 * slots, wide), bf16),
            pltpu.VMEM((2, 2 * slots, wide), f32),
            pltpu.VMEM((2, slots, wide), f32),
            pltpu.VMEM((tiles, slots, wide), bf16),
            pltpu.VMEM((tiles, slots, wide), bf16),
            dma((4,)),
            dma((2, chunks)),
            dma((3,)),
            dma((3,)),
            dma((3,)),
            dma((3,)),
        ]
        + [dma((tiles,))] * 10,
        compiler_params=pltpu.CompilerParams(
            collective_id=0, has_side_effects=True, vmem_limit_bytes=58 * 1024 * 1024
        ),
    )(mask, d_hidden, tokens, w_master)
    steps = rows // depth
    grad, tops = pl.pallas_call(
        gradient_kernel,
        name="weight_gradient",
        grid=(steps,),
        out_shape=(
            jax.ShapeDtypeStruct((rows, 2 * columns), bf16),
            jax.ShapeDtypeStruct((steps, 6, SUB, LANE), f32),
        ),
        in_specs=[
            pl.BlockSpec((4 * slots, depth), lambda d: (0, d)),
            pl.BlockSpec((tiles, 4 * slots, wide), lambda d: (0, 0, 0)),
        ],
        out_specs=(
            pl.BlockSpec((depth, 2 * columns), lambda d: (d, 0)),
            pl.BlockSpec((1, 6, SUB, LANE), lambda d: (d, 0, 0, 0)),
        ),
        scratch_shapes=[pltpu.VMEM((depth, 4 * slots), bf16)],
        compiler_params=pltpu.CompilerParams(vmem_limit_bytes=32 * 1024 * 1024),
    )(slot_cols, grads)
    block_max = lax.pmax(jnp.max(tops, axis=(2, 3)).reshape(-1), "col")
    inverse = 1.0 / (block_max + epsilon)
    update, new_master = pl.pallas_call(
        update_kernel,
        name="master_update",
        out_shape=(jax.ShapeDtypeStruct(w_master.shape, f32),) * 2,
        in_specs=[pl.BlockSpec(memory_space=pltpu.SMEM), vmem, hbm, hbm],
        out_specs=(hbm, hbm),
        scratch_shapes=[
            pltpu.VMEM((2, rows, columns), f32),
            pltpu.VMEM((2, rows, columns), f32),
            pltpu.VMEM((rows, 2 * columns), bf16),
            dma((2, blocks)),
            dma((blocks,)),
            dma((2, blocks)),
            dma((2, blocks)),
        ],
        compiler_params=pltpu.CompilerParams(vmem_limit_bytes=48 * 1024 * 1024),
    )(inverse, colmax, w_master, grad)
    return (hidden, update, new_master)


def solution(mesh):
    in_specs = (P("row", None), P("row", None), P("row", None, "col"), P("row", "col"))
    out_specs = (P("row", "col"), P("row", None, "col"), P("row", None, "col"))
    return jax.shard_map(
        on_device, mesh=mesh, in_specs=in_specs, out_specs=out_specs, check_vma=False
    )
```

```python
import jax
import jax.numpy as jnp
from jax import lax
from jax.experimental import pallas as pl
from jax.experimental.pallas import tpu as pltpu
from jax.sharding import PartitionSpec as P

BLK = 128


epsilon = 1e-06
quant_range = 448.0
learn_rate = 0.05


def on_device_plain(tokens, routes, w_master, d_hidden):
    rows_local, _, columns = w_master.shape
    slots = d_hidden.shape[0]
    colmax = lax.pmax(jnp.max(jnp.abs(w_master), axis=0), "row")
    wscale = (colmax + epsilon) / quant_range
    quantized = (w_master / wscale).astype(jnp.bfloat16).reshape(rows_local, 2 * columns)
    flat_scale = wscale.reshape(2 * columns)
    routed = jnp.any(routes == 0, axis=1)
    picked = jnp.nonzero(routed, size=slots)[0].astype(jnp.int32)
    slot_rows = tokens[picked]
    slot_cols = lax.all_to_all(slot_rows, "row", split_axis=1, concat_axis=0, tiled=True)
    slot_part = lax.slice_in_dim(slot_cols, 0, lax.axis_size("row") * slots, axis=0)
    summed = lax.psum_scatter(
        jnp.dot(slot_part, quantized, preferred_element_type=jnp.float32).astype(jnp.bfloat16),
        "row",
        scatter_dimension=0,
        tiled=True,
    ).astype(jnp.float32)
    projected = (summed * flat_scale).reshape(slots, 2, columns)
    gate_pre = projected[:, 0]
    up_pre = projected[:, 1]
    gate_sig = jax.nn.sigmoid(gate_pre)
    gate_act = gate_pre * gate_sig
    hidden = (gate_act * up_pre).astype(jnp.bfloat16)
    upstream = d_hidden.astype(jnp.float32)
    grad_gate = upstream * up_pre * gate_sig * (1.0 + gate_pre * (1.0 - gate_sig))
    grad_up = upstream * gate_act
    grad_pre = (
        jnp.stack([grad_gate, grad_up], axis=1).astype(jnp.bfloat16).reshape(slots, 2 * columns)
    )
    shard_piece = lax.all_gather(grad_pre, "row", axis=0, tiled=True)
    groups = shard_piece.shape[0] // slots
    slot_part = lax.slice_in_dim(slot_cols, 0, shard_piece.shape[0], axis=0).reshape(
        groups, slots, rows_local
    )
    block_terms = jnp.einsum(
        "gsd,gsf->gdf",
        slot_part,
        shard_piece.reshape(groups, slots, 2 * columns),
        preferred_element_type=jnp.float32,
    )
    rounded = lax.optimization_barrier(block_terms.astype(jnp.bfloat16)).astype(jnp.float32)
    grad_full = jnp.sum(rounded, axis=0)
    grad_blocks = grad_full.reshape(rows_local // BLK, BLK, 2, columns)
    block_max = lax.pmax(jnp.max(jnp.abs(grad_blocks), axis=(1, 3)), "col")
    update = (grad_blocks / (block_max[:, None, :, None] + epsilon)).reshape(rows_local, 2, columns)
    new_master = w_master - learn_rate * colmax * update
    return (hidden, update, new_master)


LANE = 128
SUB = 8


def moved(src, dst, send, recv, to, axis="row"):
    return pltpu.make_async_remote_copy(
        src_ref=src,
        dst_ref=dst,
        send_sem=send,
        recv_sem=recv,
        device_id={axis: to},
        device_id_type=pl.DeviceIdType.MESH,
    )


def forward_kernel(
    mask_ref, dh_ref, tok_hbm, w_hbm, hid_ref, grad_hbm, cm_ref, top_ref,
    sc_ref, ga_ref, turned, gbuf, tops, topx, tokv, asend, hsend, wv, folded, cmx, psend, prec, keep, own, xsend, xrec,
    tok_sem, w_sem, a_send, a_recv, y_send, y_recv, s_send, s_recv, t_send, t_recv, g_sem, c_send, c_recv, p_send, p_recv,
    x_send, x_recv, ga_send, ga_recv, gp_send, gp_recv, gf_send, gf_recv,
):
    me = lax.axis_index("row")
    core = lax.rem(me, 2)
    partner = me + 1 - 2 * core
    across = lax.rem(me + 2, 4)
    diag = lax.rem(partner + 2, 4)
    where_to = (me, across, partner, diag)
    tiles = ga_ref.shape[0]
    slots = hid_ref.shape[0]
    rows = sc_ref.shape[1]
    toks = mask_ref.shape[1]
    chunks = w_sem.shape[1]
    piece = rows // chunks

    order = (3, 1, 2, 0)
    tok_copies = {}
    for j in order:
        cols = pl.ds(pl.multiple_of(where_to[j] * rows, LANE), rows)
        tok_copies[j] = pltpu.make_async_copy(tok_hbm.at[:, cols], tokv.at[j], tok_sem.at[j])
        tok_copies[j].start()
    w_copies = []
    for k in range(chunks):
        part = pl.ds(k * piece, piece)
        for p in range(2):
            w_copies.append(
                pltpu.make_async_copy(w_hbm.at[part, p, :], wv.at[p, part], w_sem.at[p, k])
            )
            w_copies[-1].start()

    col = lax.axis_index("col")
    ncol = topx.shape[0]
    side = lax.rem(col, 2)
    beside = col + 1 - 2 * side
    half = slots // 2
    barrier = pltpu.get_barrier_semaphore()
    for d in range(1, ncol):
        pl.semaphore_signal(
            barrier,
            inc=1,
            device_id={"col": lax.rem(col + d, ncol)},
            device_id_type=pl.DeviceIdType.MESH,
        )
    for j in (1, 2, 3):
        pl.semaphore_signal(
            barrier, inc=1, device_id={"row": where_to[j]}, device_id_type=pl.DeviceIdType.MESH
        )

    mask = mask_ref[...]
    before = lax.broadcasted_iota(jnp.int32, (toks, toks), 0)
    after = lax.broadcasted_iota(jnp.int32, (toks, toks), 1)
    ladder = jnp.where(before < after, 1.0, 0.0).astype(jnp.bfloat16)
    place = jnp.dot(mask, ladder, preferred_element_type=jnp.float32)[0:1, :].astype(jnp.int32)
    flag = mask[0:1, :].astype(jnp.float32)
    slot_id = lax.broadcasted_iota(jnp.int32, (slots, toks), 0)
    pick = jnp.where(slot_id == place, flag, 0.0).astype(jnp.bfloat16)
    half_id = lax.broadcasted_iota(jnp.int32, (half, toks), 0) + side * half
    half_pick = jnp.where(half_id == place, flag, 0.0).astype(jnp.bfloat16)
    pl.semaphore_wait(barrier, 3 + ncol - 1)

    pieces = y_send.shape[1]
    wide = rows // pieces

    def segment(j, k):
        lines = pl.ds(pl.multiple_of(j * slots + side * half, half), half)
        return sc_ref.at[lines, k * wide : (k + 1) * wide]

    far = []
    for n, j in enumerate((3, 1)):
        tok_copies[j].wait()
        hsend[n] = jnp.dot(half_pick, tokv[j], preferred_element_type=jnp.float32).astype(jnp.bfloat16)
        for k in range(pieces):
            block = hsend.at[n, :, k * wide : (k + 1) * wide]
            out = moved(block, segment(j, k), y_send.at[n, k], y_recv.at[n, k], where_to[j])
            out.start()
            on = moved(segment(j, k), segment(j, k), s_send.at[n, k], s_recv.at[n, k], beside, "col")
            far.append((out, on))
    tok_copies[2].wait()
    asend[...] = jnp.dot(pick, tokv[2], preferred_element_type=jnp.float32).astype(jnp.bfloat16)
    near = moved(asend, sc_ref.at[pl.ds(2 * slots, slots)], a_send, a_recv, partner)
    near.start()
    tok_copies[0].wait()
    sc_ref[0:slots, :] = jnp.dot(pick, tokv[0], preferred_element_type=jnp.float32).astype(jnp.bfloat16)

    folded[...] = jnp.zeros(folded.shape, jnp.float32)
    for k in range(chunks):
        for p in range(2):
            w_copies[2 * k + p].wait()

        def fold(t, carry, k=k):
            cols = pl.ds(pl.multiple_of(t * LANE, LANE), LANE)
            for p in range(2):
                tile = jnp.abs(wv[p, k * piece : (k + 1) * piece, cols])
                best = jnp.max(tile.reshape(-1, SUB, LANE), axis=0)
                folded[p, :, cols] = jnp.maximum(folded[p, :, cols], best)
            return carry

        lax.fori_loop(0, tiles, fold, 0)
        far[k][0].wait_recv()
        far[k][1].start()
    cmx[0] = jnp.zeros(cmx.shape[1:], jnp.float32)
    for p in range(2):
        cmx[0, p : p + 1, :] = jnp.max(folded[p], axis=0, keepdims=True)
    c_copies = []
    for j in (1, 2, 3):
        c_copies.append(moved(cmx.at[0], cmx.at[j], c_send.at[j - 1], c_recv.at[j - 1], where_to[j]))
        c_copies[-1].start()
    for out, on in far[chunks:]:
        out.wait_recv()
        on.start()
    for copy in c_copies:
        copy.wait()
    cm_ref[...] = jnp.maximum(jnp.maximum(cmx[0], cmx[1]), jnp.maximum(cmx[2], cmx[3]))
    near.wait()
    for out, on in far:
        out.wait_send()
        on.wait()
    tops[...] = jnp.zeros(tops.shape, jnp.float32)
    blocks = tops.shape[0] // 2

    def scale_row(t, p):
        cols = pl.ds(pl.multiple_of(t * LANE, LANE), LANE)
        return (cm_ref[p : p + 1, cols] + epsilon) / quant_range

    def swap(t):
        return moved(psend.at[t], prec.at[t], p_send.at[t], p_recv.at[t], partner)

    def cross(t):
        return moved(xsend.at[t], xrec.at[t], x_send.at[t], x_recv.at[t], across)

    def grad_block(t, j):
        return ga_ref.at[t, pl.ds(j * slots, slots)]

    def share_across(t):
        return moved(grad_block(t, 0), grad_block(t, 1), ga_send.at[t], ga_recv.at[t], across)

    def share_partner(t):
        return moved(grad_block(t, 0), grad_block(t, 2), gp_send.at[t], gp_recv.at[t], partner)

    def forward(t):
        return moved(grad_block(t, 1), grad_block(t, 3), gf_send.at[t], gf_recv.at[t], partner)

    def put_grad(t):
        return pltpu.make_async_copy(gbuf.at[t], grad_hbm.at[t], g_sem.at[t])

    def step(i, carry):
        @pl.when(i < tiles)
        def _():
            t = i
            halves = []
            for p in range(2):
                w = wv[p, :, pl.ds(pl.multiple_of(t * LANE, LANE), LANE)]
                halves.append((w * (1.0 / scale_row(t, p))).astype(jnp.bfloat16))
            quantized = jnp.concatenate(halves, axis=1)
            term = jnp.dot(sc_ref[...], quantized, preferred_element_type=jnp.float32)
            slot = lax.rem(t, 2)
            psend[t] = term[2 * slots :].astype(jnp.bfloat16)
            keep[slot] = term[: 2 * slots]
            swap(t).start()

        @pl.when(jnp.logical_and(i >= 1, i < tiles + 1))
        def _():
            t = i - 1
            slot = lax.rem(t, 2)
            swap(t).wait_recv()
            own[slot] = keep[slot, :slots] + prec[t, :slots].astype(jnp.float32)
            xsend[t] = (keep[slot, slots:] + prec[t, slots:].astype(jnp.float32)).astype(jnp.bfloat16)
            cross(t).start()

        @pl.when(jnp.logical_and(i >= 2, i < tiles + 2))
        def _():
            t = i - 2
            cross(t).wait_recv()
            total = own[lax.rem(t, 2)] + xrec[t].astype(jnp.float32)
            gate_pre = total[:, :LANE] * scale_row(t, 0)
            up_pre = total[:, LANE:] * scale_row(t, 1)
            gate_sig = jax.nn.sigmoid(gate_pre)
            gate_act = gate_pre * gate_sig
            cols = pl.ds(pl.multiple_of(t * LANE, LANE), LANE)
            hid_ref[:, cols] = (gate_act * up_pre).astype(jnp.bfloat16)
            upstream = dh_ref[:, cols].astype(jnp.float32)
            grad_gate = upstream * up_pre * gate_sig * (1.0 + gate_pre * (1.0 - gate_sig))
            grad_up = upstream * gate_act
            ga_ref[t, 0:slots, :] = jnp.concatenate([grad_gate, grad_up], axis=1).astype(jnp.bfloat16)
            share_across(t).start()
            share_partner(t).start()

        @pl.when(jnp.logical_and(i >= 3, i < tiles + 3))
        def _():
            t = i - 3
            share_across(t).wait_recv()
            forward(t).start()

        @pl.when(i < 4)
        def _():
            part = pl.ds(pl.multiple_of(i * (rows // 4), LANE), rows // 4)
            turned[part, :] = sc_ref[:, part].T

        @pl.when(i >= 4)
        def _():
            t = i - 4
            share_partner(t).wait_recv()
            forward(t).wait_recv()
            grad = jnp.dot(turned[...], ga_ref[t], preferred_element_type=jnp.float32)
            gbuf[t] = grad.astype(jnp.bfloat16)
            for b in range(blocks):
                for p in range(2):
                    tile = jnp.abs(grad[b * BLK : (b + 1) * BLK, p * LANE : (p + 1) * LANE])
                    best = jnp.max(tile.reshape(-1, SUB, LANE), axis=0)
                    tops[2 * b + p] = jnp.maximum(tops[2 * b + p], best)
            put_grad(t).start()

        return carry

    lax.fori_loop(0, tiles + 4, step, 0)

    topx[0] = jnp.max(tops[...], axis=1)
    t_copies = []
    for d in range(1, ncol):
        t_copies.append(
            moved(topx.at[0], topx.at[d], t_send.at[d], t_recv.at[d], lax.rem(col + d, ncol), "col")
        )
        t_copies[-1].start()

    def finish(t, carry):
        swap(t).wait_send()
        cross(t).wait_send()
        share_across(t).wait_send()
        share_partner(t).wait_send()
        forward(t).wait_send()
        put_grad(t).wait()
        return carry

    lax.fori_loop(0, tiles, finish, 0)
    for copy in t_copies:
        copy.wait()
    top = topx[0]
    for d in range(1, ncol):
        top = jnp.maximum(top, topx[d])
    top_ref[...] = jnp.broadcast_to(jnp.max(top, axis=1, keepdims=True), top_ref.shape)


def update_kernel(inv_ref, cm_ref, w_hbm, grad_hbm, update_hbm, new_hbm, wv, uv, gv, w_sem, g_sem, u_sem, n_sem):
    blocks = g_sem.shape[0]
    columns = wv.shape[2]
    tiles = columns // LANE

    def part(b):
        return pl.ds(pl.multiple_of(b * BLK, BLK), BLK)

    def old(b, p):
        return pltpu.make_async_copy(w_hbm.at[part(b), p, :], wv.at[p, part(b)], w_sem.at[p, b])

    def gradient(b):
        return pltpu.make_async_copy(grad_hbm.at[:, part(b)], gv.at[:, part(b)], g_sem.at[b])

    def put_update(b, p):
        return pltpu.make_async_copy(uv.at[p, part(b)], update_hbm.at[part(b), p, :], u_sem.at[p, b])

    def put_new(b, p):
        return pltpu.make_async_copy(wv.at[p, part(b)], new_hbm.at[part(b), p, :], n_sem.at[p, b])

    def begin(b, carry):
        gradient(b).start()
        for p in range(2):
            old(b, p).start()
        return carry

    def step(b, carry):
        gradient(b).wait()
        for p in range(2):
            old(b, p).wait()
            inverse = inv_ref[2 * b + p]
            for t in range(tiles):
                cols = slice(t * LANE, (t + 1) * LANE)
                update = gv[t, part(b), p * LANE : (p + 1) * LANE].astype(jnp.float32) * inverse
                uv[p, part(b), cols] = update
                wv[p, part(b), cols] = wv[p, part(b), cols] - (learn_rate * cm_ref[p : p + 1, cols]) * update
            put_update(b, p).start()
            put_new(b, p).start()
        return carry

    def finish(b, carry):
        for p in range(2):
            put_update(b, p).wait()
            put_new(b, p).wait()
        return carry

    lax.fori_loop(0, blocks, begin, 0)
    lax.fori_loop(0, blocks, step, 0)
    lax.fori_loop(0, blocks, finish, 0)


def on_device(tokens, routes, w_master, d_hidden):
    rows, _, columns = w_master.shape
    slots = d_hidden.shape[0]
    toks = tokens.shape[0]
    ncol = lax.axis_size("col")
    aligned = columns % LANE == 0 and rows % (4 * BLK) == 0 and slots % 32 == 0 and toks % LANE == 0
    if lax.axis_size("row") != 4 or ncol % 2 or not aligned:
        return on_device_plain(tokens, routes, w_master, d_hidden)
    tiles = columns // LANE
    bf16, f32 = jnp.bfloat16, jnp.float32
    routed = jnp.any(routes == 0, axis=1).astype(bf16)
    mask = jnp.broadcast_to(routed[None, :], (16, toks))
    chunks = 4
    pieces = 4
    blocks = rows // BLK
    vmem = pl.BlockSpec(memory_space=pltpu.VMEM)
    hbm = pl.BlockSpec(memory_space=pl.ANY)
    dma = pltpu.SemaphoreType.DMA
    wide = 2 * LANE
    hidden, grad, colmax, tops = pl.pallas_call(
        forward_kernel,
        name="forward_exchange",
        out_shape=(
            jax.ShapeDtypeStruct((slots, columns), bf16),
            jax.ShapeDtypeStruct((tiles, rows, wide), bf16),
            jax.ShapeDtypeStruct((SUB, columns), f32),
            jax.ShapeDtypeStruct((2 * blocks, LANE), f32),
        ),
        in_specs=[vmem, vmem, hbm, hbm],
        out_specs=(vmem, hbm, vmem, vmem),
        scratch_shapes=[
            pltpu.VMEM((4 * slots, rows), bf16),
            pltpu.VMEM((tiles, 4 * slots, wide), bf16),
            pltpu.VMEM((rows, 4 * slots), bf16),
            pltpu.VMEM((tiles, rows, wide), bf16),
            pltpu.VMEM((2 * blocks, SUB, LANE), f32),
            pltpu.VMEM((ncol, 2 * blocks, LANE), f32),
            pltpu.VMEM((4, toks, rows), bf16),
            pltpu.VMEM((slots, rows), bf16),
            pltpu.VMEM((2, slots // 2, rows), bf16),
            pltpu.VMEM((2, rows, columns), f32),
            pltpu.VMEM((2, SUB, columns), f32),
            pltpu.VMEM((4, SUB, columns), f32),
            pltpu.VMEM((tiles, 2 * slots, wide), bf16),
            pltpu.VMEM((tiles, 2 * slots, wide), bf16),
            pltpu.VMEM((2, 2 * slots, wide), f32),
            pltpu.VMEM((2, slots, wide), f32),
            pltpu.VMEM((tiles, slots, wide), bf16),
            pltpu.VMEM((tiles, slots, wide), bf16),
            dma((4,)),
            dma((2, chunks)),
            dma,
            dma,
            dma((2, pieces)),
            dma((2, pieces)),
            dma((2, pieces)),
            dma((2, pieces)),
            dma((ncol,)),
            dma((ncol,)),
            dma((tiles,)),
            dma((3,)),
            dma((3,)),
        ]
        + [dma((tiles,))] * 10,
        compiler_params=pltpu.CompilerParams(
            collective_id=0, has_side_effects=True, vmem_limit_bytes=58 * 1024 * 1024
        ),
    )(mask, d_hidden, tokens, w_master)
    inverse = 1.0 / (tops[:, 0] + epsilon)
    update, new_master = pl.pallas_call(
        update_kernel,
        name="master_update",
        out_shape=(jax.ShapeDtypeStruct(w_master.shape, f32),) * 2,
        in_specs=[pl.BlockSpec(memory_space=pltpu.SMEM), vmem, hbm, hbm],
        out_specs=(hbm, hbm),
        scratch_shapes=[
            pltpu.VMEM((2, rows, columns), f32),
            pltpu.VMEM((2, rows, columns), f32),
            pltpu.VMEM((tiles, rows, wide), bf16),
            dma((2, blocks)),
            dma((blocks,)),
            dma((2, blocks)),
            dma((2, blocks)),
        ],
        compiler_params=pltpu.CompilerParams(vmem_limit_bytes=48 * 1024 * 1024),
    )(inverse, colmax, w_master, grad)
    return (hidden, update, new_master)


def solution(mesh):
    in_specs = (P("row", None), P("row", None), P("row", None, "col"), P("row", "col"))
    out_specs = (P("row", "col"), P("row", None, "col"), P("row", None, "col"))
    return jax.shard_map(
        on_device, mesh=mesh, in_specs=in_specs, out_specs=out_specs, check_vma=False
    )
```

```python
import jax
import jax.numpy as jnp
from jax import lax
from jax.experimental import pallas as pl
from jax.experimental.pallas import tpu as pltpu
from jax.sharding import PartitionSpec as P

BLK = 128


epsilon = 1e-06
quant_range = 448.0
learn_rate = 0.05


def on_device_plain(tokens, routes, w_master, d_hidden):
    rows_local, _, columns = w_master.shape
    slots = d_hidden.shape[0]
    colmax = lax.pmax(jnp.max(jnp.abs(w_master), axis=0), "row")
    wscale = (colmax + epsilon) / quant_range
    quantized = (w_master / wscale).astype(jnp.bfloat16).reshape(rows_local, 2 * columns)
    flat_scale = wscale.reshape(2 * columns)
    routed = jnp.any(routes == 0, axis=1)
    picked = jnp.nonzero(routed, size=slots)[0].astype(jnp.int32)
    slot_rows = tokens[picked]
    slot_cols = lax.all_to_all(slot_rows, "row", split_axis=1, concat_axis=0, tiled=True)
    slot_part = lax.slice_in_dim(slot_cols, 0, lax.axis_size("row") * slots, axis=0)
    summed = lax.psum_scatter(
        jnp.dot(slot_part, quantized, preferred_element_type=jnp.float32).astype(jnp.bfloat16),
        "row",
        scatter_dimension=0,
        tiled=True,
    ).astype(jnp.float32)
    projected = (summed * flat_scale).reshape(slots, 2, columns)
    gate_pre = projected[:, 0]
    up_pre = projected[:, 1]
    gate_sig = jax.nn.sigmoid(gate_pre)
    gate_act = gate_pre * gate_sig
    hidden = (gate_act * up_pre).astype(jnp.bfloat16)
    upstream = d_hidden.astype(jnp.float32)
    grad_gate = upstream * up_pre * gate_sig * (1.0 + gate_pre * (1.0 - gate_sig))
    grad_up = upstream * gate_act
    grad_pre = (
        jnp.stack([grad_gate, grad_up], axis=1).astype(jnp.bfloat16).reshape(slots, 2 * columns)
    )
    shard_piece = lax.all_gather(grad_pre, "row", axis=0, tiled=True)
    groups = shard_piece.shape[0] // slots
    slot_part = lax.slice_in_dim(slot_cols, 0, shard_piece.shape[0], axis=0).reshape(
        groups, slots, rows_local
    )
    block_terms = jnp.einsum(
        "gsd,gsf->gdf",
        slot_part,
        shard_piece.reshape(groups, slots, 2 * columns),
        preferred_element_type=jnp.float32,
    )
    rounded = lax.optimization_barrier(block_terms.astype(jnp.bfloat16)).astype(jnp.float32)
    grad_full = jnp.sum(rounded, axis=0)
    grad_blocks = grad_full.reshape(rows_local // BLK, BLK, 2, columns)
    block_max = lax.pmax(jnp.max(jnp.abs(grad_blocks), axis=(1, 3)), "col")
    update = (grad_blocks / (block_max[:, None, :, None] + epsilon)).reshape(rows_local, 2, columns)
    new_master = w_master - learn_rate * colmax * update
    return (hidden, update, new_master)


LANE = 128
SUB = 8


def moved(src, dst, send, recv, to, axis="row"):
    return pltpu.make_async_remote_copy(
        src_ref=src,
        dst_ref=dst,
        send_sem=send,
        recv_sem=recv,
        device_id={axis: to},
        device_id_type=pl.DeviceIdType.MESH,
    )


def forward_kernel(
    routes_ref, dh_ref, tok_hbm, w_hbm, hid_ref, gbuf, wv, cm_ref, top_ref,
    sc_ref, ga_ref, turned, tops, topx, tokv, asend, hsend, folded, cmx, psend, prec, keep, own, xsend, xrec,
    tok_sem, w_sem, a_send, a_recv, y_send, y_recv, s_send, s_recv, t_send, t_recv, c_send, c_recv, p_send, p_recv,
    x_send, x_recv, ga_send, ga_recv, gp_send, gp_recv, gf_send, gf_recv,
):
    me = lax.axis_index("row")
    core = lax.rem(me, 2)
    partner = me + 1 - 2 * core
    across = lax.rem(me + 2, 4)
    diag = lax.rem(partner + 2, 4)
    where_to = (me, across, partner, diag)
    tiles = ga_ref.shape[0]
    slots = hid_ref.shape[0]
    rows = sc_ref.shape[1]
    toks = routes_ref.shape[1]
    chunks = w_sem.shape[1]
    piece = rows // chunks

    order = (3, 1, 2, 0)
    tok_copies = {}
    for j in order:
        cols = pl.ds(pl.multiple_of(where_to[j] * rows, LANE), rows)
        tok_copies[j] = pltpu.make_async_copy(tok_hbm.at[:, cols], tokv.at[j], tok_sem.at[j])
        tok_copies[j].start()
    w_copies = []
    for k in range(chunks):
        part = pl.ds(k * piece, piece)
        for p in range(2):
            w_copies.append(
                pltpu.make_async_copy(w_hbm.at[part, p, :], wv.at[p, part], w_sem.at[p, k])
            )
            w_copies[-1].start()

    col = lax.axis_index("col")
    ncol = topx.shape[0]
    side = lax.rem(col, 2)
    beside = col + 1 - 2 * side
    half = slots // 2
    barrier = pltpu.get_barrier_semaphore()
    for d in range(1, ncol):
        pl.semaphore_signal(
            barrier,
            inc=1,
            device_id={"col": lax.rem(col + d, ncol)},
            device_id_type=pl.DeviceIdType.MESH,
        )
    for j in (1, 2, 3):
        pl.semaphore_signal(
            barrier, inc=1, device_id={"row": where_to[j]}, device_id_type=pl.DeviceIdType.MESH
        )

    named = jnp.logical_or(routes_ref[0:1, :] == 0, routes_ref[1:2, :] == 0)
    flag = jnp.where(named, 1.0, 0.0)
    mask = jnp.broadcast_to(flag, (16, toks)).astype(jnp.bfloat16)
    before = lax.broadcasted_iota(jnp.int32, (toks, toks), 0)
    after = lax.broadcasted_iota(jnp.int32, (toks, toks), 1)
    ladder = jnp.where(before < after, 1.0, 0.0).astype(jnp.bfloat16)
    place = jnp.dot(mask, ladder, preferred_element_type=jnp.float32)[0:1, :].astype(jnp.int32)
    slot_id = lax.broadcasted_iota(jnp.int32, (slots, toks), 0)
    pick = jnp.where(slot_id == place, flag, 0.0).astype(jnp.bfloat16)
    half_id = lax.broadcasted_iota(jnp.int32, (half, toks), 0) + side * half
    half_pick = jnp.where(half_id == place, flag, 0.0).astype(jnp.bfloat16)
    pl.semaphore_wait(barrier, 3 + ncol - 1)

    pieces = y_send.shape[1]
    wide = rows // pieces

    def segment(j, k):
        lines = pl.ds(pl.multiple_of(j * slots + side * half, half), half)
        return sc_ref.at[lines, k * wide : (k + 1) * wide]

    far = []
    for n, j in enumerate((3, 1)):
        tok_copies[j].wait()
        hsend[n] = jnp.dot(half_pick, tokv[j], preferred_element_type=jnp.float32).astype(jnp.bfloat16)
        for k in range(pieces):
            block = hsend.at[n, :, k * wide : (k + 1) * wide]
            out = moved(block, segment(j, k), y_send.at[n, k], y_recv.at[n, k], where_to[j])
            out.start()
            on = moved(segment(j, k), segment(j, k), s_send.at[n, k], s_recv.at[n, k], beside, "col")
            far.append((out, on))
    tok_copies[2].wait()
    asend[...] = jnp.dot(pick, tokv[2], preferred_element_type=jnp.float32).astype(jnp.bfloat16)
    near = moved(asend, sc_ref.at[pl.ds(2 * slots, slots)], a_send, a_recv, partner)
    near.start()
    tok_copies[0].wait()
    sc_ref[0:slots, :] = jnp.dot(pick, tokv[0], preferred_element_type=jnp.float32).astype(jnp.bfloat16)

    folded[...] = jnp.zeros(folded.shape, jnp.float32)
    for k in range(chunks):
        for p in range(2):
            w_copies[2 * k + p].wait()

        def fold(t, carry, k=k):
            cols = pl.ds(pl.multiple_of(t * LANE, LANE), LANE)
            for p in range(2):
                tile = jnp.abs(wv[p, k * piece : (k + 1) * piece, cols])
                best = jnp.max(tile.reshape(-1, SUB, LANE), axis=0)
                folded[p, :, cols] = jnp.maximum(folded[p, :, cols], best)
            return carry

        lax.fori_loop(0, tiles, fold, 0)
        far[k][0].wait_recv()
        far[k][1].start()
    cmx[0] = jnp.zeros(cmx.shape[1:], jnp.float32)
    for p in range(2):
        cmx[0, p : p + 1, :] = jnp.max(folded[p], axis=0, keepdims=True)
    c_copies = []
    for j in (1, 2, 3):
        c_copies.append(moved(cmx.at[0], cmx.at[j], c_send.at[j - 1], c_recv.at[j - 1], where_to[j]))
        c_copies[-1].start()
    for out, on in far[chunks:]:
        out.wait_recv()
        on.start()
    for copy in c_copies:
        copy.wait()
    cm_ref[...] = jnp.maximum(jnp.maximum(cmx[0], cmx[1]), jnp.maximum(cmx[2], cmx[3]))
    near.wait()
    for out, on in far:
        out.wait_send()
        on.wait()
    tops[...] = jnp.zeros(tops.shape, jnp.float32)
    blocks = tops.shape[0] // 2

    def scale_row(t, p):
        cols = pl.ds(pl.multiple_of(t * LANE, LANE), LANE)
        return (cm_ref[p : p + 1, cols] + epsilon) / quant_range

    def swap(t):
        return moved(psend.at[t], prec.at[t], p_send.at[t], p_recv.at[t], partner)

    def cross(t):
        return moved(xsend.at[t], xrec.at[t], x_send.at[t], x_recv.at[t], across)

    def grad_block(t, j):
        return ga_ref.at[t, pl.ds(j * slots, slots)]

    def share_across(t):
        return moved(grad_block(t, 0), grad_block(t, 1), ga_send.at[t], ga_recv.at[t], across)

    def share_partner(t):
        return moved(grad_block(t, 0), grad_block(t, 2), gp_send.at[t], gp_recv.at[t], partner)

    def forward(t):
        return moved(grad_block(t, 1), grad_block(t, 3), gf_send.at[t], gf_recv.at[t], partner)

    def step(i, carry):
        @pl.when(i < tiles)
        def _():
            t = i
            halves = []
            for p in range(2):
                w = wv[p, :, pl.ds(pl.multiple_of(t * LANE, LANE), LANE)]
                halves.append((w * (1.0 / scale_row(t, p))).astype(jnp.bfloat16))
            quantized = jnp.concatenate(halves, axis=1)
            term = jnp.dot(sc_ref[...], quantized, preferred_element_type=jnp.float32)
            slot = lax.rem(t, 2)
            psend[t] = term[2 * slots :].astype(jnp.bfloat16)
            keep[slot] = term[: 2 * slots]
            swap(t).start()

        @pl.when(jnp.logical_and(i >= 1, i < tiles + 1))
        def _():
            t = i - 1
            slot = lax.rem(t, 2)
            swap(t).wait_recv()
            own[slot] = keep[slot, :slots] + prec[t, :slots].astype(jnp.float32)
            xsend[t] = (keep[slot, slots:] + prec[t, slots:].astype(jnp.float32)).astype(jnp.bfloat16)
            cross(t).start()

        @pl.when(jnp.logical_and(i >= 2, i < tiles + 2))
        def _():
            t = i - 2
            cross(t).wait_recv()
            total = own[lax.rem(t, 2)] + xrec[t].astype(jnp.float32)
            gate_pre = total[:, :LANE] * scale_row(t, 0)
            up_pre = total[:, LANE:] * scale_row(t, 1)
            gate_sig = jax.nn.sigmoid(gate_pre)
            gate_act = gate_pre * gate_sig
            cols = pl.ds(pl.multiple_of(t * LANE, LANE), LANE)
            hid_ref[:, cols] = (gate_act * up_pre).astype(jnp.bfloat16)
            upstream = dh_ref[:, cols].astype(jnp.float32)
            grad_gate = upstream * up_pre * gate_sig * (1.0 + gate_pre * (1.0 - gate_sig))
            grad_up = upstream * gate_act
            ga_ref[t, 0:slots, :] = jnp.concatenate([grad_gate, grad_up], axis=1).astype(jnp.bfloat16)
            share_across(t).start()
            share_partner(t).start()

        @pl.when(jnp.logical_and(i >= 3, i < tiles + 3))
        def _():
            t = i - 3
            share_across(t).wait_recv()
            forward(t).start()

        @pl.when(i < 4)
        def _():
            part = pl.ds(pl.multiple_of(i * (rows // 4), LANE), rows // 4)
            turned[part, :] = sc_ref[:, part].T

        @pl.when(i >= 4)
        def _():
            t = i - 4
            share_partner(t).wait_recv()
            forward(t).wait_recv()
            grad = jnp.dot(turned[...], ga_ref[t], preferred_element_type=jnp.float32)
            gbuf[t] = grad.astype(jnp.bfloat16)
            for b in range(blocks):
                for p in range(2):
                    tile = jnp.abs(grad[b * BLK : (b + 1) * BLK, p * LANE : (p + 1) * LANE])
                    best = jnp.max(tile.reshape(-1, SUB, LANE), axis=0)
                    tops[2 * b + p] = jnp.maximum(tops[2 * b + p], best)

        return carry

    lax.fori_loop(0, tiles + 4, step, 0)

    topx[0] = jnp.max(tops[...], axis=1)
    t_copies = []
    for d in range(1, ncol):
        t_copies.append(
            moved(topx.at[0], topx.at[d], t_send.at[d], t_recv.at[d], lax.rem(col + d, ncol), "col")
        )
        t_copies[-1].start()

    def finish(t, carry):
        swap(t).wait_send()
        cross(t).wait_send()
        share_across(t).wait_send()
        share_partner(t).wait_send()
        forward(t).wait_send()
        return carry

    lax.fori_loop(0, tiles, finish, 0)
    for copy in t_copies:
        copy.wait()
    top = topx[0]
    for d in range(1, ncol):
        top = jnp.maximum(top, topx[d])
    top_ref[...] = jnp.broadcast_to(jnp.max(top, axis=1, keepdims=True), top_ref.shape)


def update_kernel(inv_ref, cm_ref, wv, gv, update_hbm, new_hbm, uv, nv, u_sem, n_sem):
    blocks = u_sem.shape[1]
    tiles = gv.shape[0]

    def part(b):
        return pl.ds(pl.multiple_of(b * BLK, BLK), BLK)

    def put_update(b, p):
        return pltpu.make_async_copy(uv.at[p, part(b)], update_hbm.at[part(b), p, :], u_sem.at[p, b])

    def put_new(b, p):
        return pltpu.make_async_copy(nv.at[p, part(b)], new_hbm.at[part(b), p, :], n_sem.at[p, b])

    def step(b, carry):
        for p in range(2):
            inverse = inv_ref[2 * b + p]
            for t in range(tiles):
                cols = slice(t * LANE, (t + 1) * LANE)
                update = gv[t, part(b), p * LANE : (p + 1) * LANE].astype(jnp.float32) * inverse
                uv[p, part(b), cols] = update
                nv[p, part(b), cols] = wv[p, part(b), cols] - (learn_rate * cm_ref[p : p + 1, cols]) * update
            put_update(b, p).start()
            put_new(b, p).start()
        return carry

    def finish(b, carry):
        for p in range(2):
            put_update(b, p).wait()
            put_new(b, p).wait()
        return carry

    lax.fori_loop(0, blocks, step, 0)
    lax.fori_loop(0, blocks, finish, 0)


def on_device(tokens, routes, w_master, d_hidden):
    rows, _, columns = w_master.shape
    slots = d_hidden.shape[0]
    toks = tokens.shape[0]
    ncol = lax.axis_size("col")
    aligned = columns % LANE == 0 and rows % (4 * BLK) == 0 and slots % 32 == 0 and toks % LANE == 0
    if lax.axis_size("row") != 4 or ncol % 2 or not aligned:
        return on_device_plain(tokens, routes, w_master, d_hidden)
    tiles = columns // LANE
    bf16, f32 = jnp.bfloat16, jnp.float32
    chunks = 4
    pieces = 4
    blocks = rows // BLK
    vmem = pl.BlockSpec(memory_space=pltpu.VMEM)
    hbm = pl.BlockSpec(memory_space=pl.ANY)
    dma = pltpu.SemaphoreType.DMA
    wide = 2 * LANE
    hidden, grad, halves, colmax, tops = pl.pallas_call(
        forward_kernel,
        name="forward_exchange",
        out_shape=(
            jax.ShapeDtypeStruct((slots, columns), bf16),
            pltpu.VMEM((tiles, rows, wide), bf16),
            pltpu.VMEM((2, rows, columns), f32),
            jax.ShapeDtypeStruct((SUB, columns), f32),
            jax.ShapeDtypeStruct((2 * blocks, LANE), f32),
        ),
        in_specs=[vmem, vmem, hbm, hbm],
        out_specs=(vmem, vmem, vmem, vmem, vmem),
        scratch_shapes=[
            pltpu.VMEM((4 * slots, rows), bf16),
            pltpu.VMEM((tiles, 4 * slots, wide), bf16),
            pltpu.VMEM((rows, 4 * slots), bf16),
            pltpu.VMEM((2 * blocks, SUB, LANE), f32),
            pltpu.VMEM((ncol, 2 * blocks, LANE), f32),
            pltpu.VMEM((4, toks, rows), bf16),
            pltpu.VMEM((slots, rows), bf16),
            pltpu.VMEM((2, slots // 2, rows), bf16),
            pltpu.VMEM((2, SUB, columns), f32),
            pltpu.VMEM((4, SUB, columns), f32),
            pltpu.VMEM((tiles, 2 * slots, wide), bf16),
            pltpu.VMEM((tiles, 2 * slots, wide), bf16),
            pltpu.VMEM((2, 2 * slots, wide), f32),
            pltpu.VMEM((2, slots, wide), f32),
            pltpu.VMEM((tiles, slots, wide), bf16),
            pltpu.VMEM((tiles, slots, wide), bf16),
            dma((4,)),
            dma((2, chunks)),
            dma,
            dma,
            dma((2, pieces)),
            dma((2, pieces)),
            dma((2, pieces)),
            dma((2, pieces)),
            dma((ncol,)),
            dma((ncol,)),
            dma((3,)),
            dma((3,)),
        ]
        + [dma((tiles,))] * 10,
        compiler_params=pltpu.CompilerParams(
            collective_id=0, has_side_effects=True, vmem_limit_bytes=38 * 1024 * 1024
        ),
    )(routes.T, d_hidden, tokens, w_master)
    inverse = 1.0 / (tops[:, 0] + epsilon)
    update, new_master = pl.pallas_call(
        update_kernel,
        name="master_update",
        out_shape=(jax.ShapeDtypeStruct(w_master.shape, f32),) * 2,
        in_specs=[pl.BlockSpec(memory_space=pltpu.SMEM), vmem, vmem, vmem],
        out_specs=(hbm, hbm),
        scratch_shapes=[
            pltpu.VMEM((2, rows, columns), f32),
            pltpu.VMEM((2, rows, columns), f32),
            dma((2, blocks)),
            dma((2, blocks)),
        ],
        compiler_params=pltpu.CompilerParams(vmem_limit_bytes=30 * 1024 * 1024),
    )(
        inverse,
        colmax,
        pltpu.with_memory_space_constraint(halves, pltpu.VMEM),
        pltpu.with_memory_space_constraint(grad, pltpu.VMEM),
    )
    return (hidden, update, new_master)


def solution(mesh):
    in_specs = (P("row", None), P("row", None), P("row", None, "col"), P("row", "col"))
    out_specs = (P("row", "col"), P("row", None, "col"), P("row", None, "col"))
    return jax.shard_map(
        on_device, mesh=mesh, in_specs=in_specs, out_specs=out_specs, check_vma=False
    )
```

```python
import jax
import jax.numpy as jnp
from jax import lax
from jax.experimental import pallas as pl
from jax.experimental.pallas import tpu as pltpu
from jax.sharding import PartitionSpec as P

BLK = 128


epsilon = 1e-06
quant_range = 448.0
learn_rate = 0.05


def on_device_plain(tokens, routes, w_master, d_hidden):
    rows_local, _, columns = w_master.shape
    slots = d_hidden.shape[0]
    colmax = lax.pmax(jnp.max(jnp.abs(w_master), axis=0), "row")
    wscale = (colmax + epsilon) / quant_range
    quantized = (w_master / wscale).astype(jnp.bfloat16).reshape(rows_local, 2 * columns)
    flat_scale = wscale.reshape(2 * columns)
    routed = jnp.any(routes == 0, axis=1)
    picked = jnp.nonzero(routed, size=slots)[0].astype(jnp.int32)
    slot_rows = tokens[picked]
    slot_cols = lax.all_to_all(slot_rows, "row", split_axis=1, concat_axis=0, tiled=True)
    slot_part = lax.slice_in_dim(slot_cols, 0, lax.axis_size("row") * slots, axis=0)
    summed = lax.psum_scatter(
        jnp.dot(slot_part, quantized, preferred_element_type=jnp.float32).astype(jnp.bfloat16),
        "row",
        scatter_dimension=0,
        tiled=True,
    ).astype(jnp.float32)
    projected = (summed * flat_scale).reshape(slots, 2, columns)
    gate_pre = projected[:, 0]
    up_pre = projected[:, 1]
    gate_sig = jax.nn.sigmoid(gate_pre)
    gate_act = gate_pre * gate_sig
    hidden = (gate_act * up_pre).astype(jnp.bfloat16)
    upstream = d_hidden.astype(jnp.float32)
    grad_gate = upstream * up_pre * gate_sig * (1.0 + gate_pre * (1.0 - gate_sig))
    grad_up = upstream * gate_act
    grad_pre = (
        jnp.stack([grad_gate, grad_up], axis=1).astype(jnp.bfloat16).reshape(slots, 2 * columns)
    )
    shard_piece = lax.all_gather(grad_pre, "row", axis=0, tiled=True)
    groups = shard_piece.shape[0] // slots
    slot_part = lax.slice_in_dim(slot_cols, 0, shard_piece.shape[0], axis=0).reshape(
        groups, slots, rows_local
    )
    block_terms = jnp.einsum(
        "gsd,gsf->gdf",
        slot_part,
        shard_piece.reshape(groups, slots, 2 * columns),
        preferred_element_type=jnp.float32,
    )
    rounded = lax.optimization_barrier(block_terms.astype(jnp.bfloat16)).astype(jnp.float32)
    grad_full = jnp.sum(rounded, axis=0)
    grad_blocks = grad_full.reshape(rows_local // BLK, BLK, 2, columns)
    block_max = lax.pmax(jnp.max(jnp.abs(grad_blocks), axis=(1, 3)), "col")
    update = (grad_blocks / (block_max[:, None, :, None] + epsilon)).reshape(rows_local, 2, columns)
    new_master = w_master - learn_rate * colmax * update
    return (hidden, update, new_master)


LANE = 128
SUB = 8


def moved(src, dst, send, recv, to, axis="row"):
    return pltpu.make_async_remote_copy(
        src_ref=src,
        dst_ref=dst,
        send_sem=send,
        recv_sem=recv,
        device_id={axis: to},
        device_id_type=pl.DeviceIdType.MESH,
    )


def forward_kernel(
    routes_ref, dh_ref, tok_hbm, w_hbm, hid_ref, gbuf, wv, cm_ref, top_ref,
    sc_ref, ga_ref, turned, tops, topx, tokv, asend, hsend, folded, cmx, psend, prec, keep, own, xsend, xrec,
    tok_sem, w_sem, a_send, a_recv, y_send, y_recv, s_send, s_recv, t_send, t_recv, c_send, c_recv, p_send, p_recv,
    x_send, x_recv, ga_send, ga_recv, gp_send, gp_recv, gf_send, gf_recv,
):
    me = lax.axis_index("row")
    core = lax.rem(me, 2)
    partner = me + 1 - 2 * core
    across = lax.rem(me + 2, 4)
    diag = lax.rem(partner + 2, 4)
    where_to = (me, across, partner, diag)
    tiles = ga_ref.shape[0]
    slots = hid_ref.shape[0]
    rows = sc_ref.shape[1]
    toks = routes_ref.shape[1]
    chunks = w_sem.shape[1]
    piece = rows // chunks

    order = (3, 1, 2, 0)
    tok_copies = {}
    for j in order:
        cols = pl.ds(pl.multiple_of(where_to[j] * rows, LANE), rows)
        tok_copies[j] = pltpu.make_async_copy(tok_hbm.at[:, cols], tokv.at[j], tok_sem.at[j])
    for j in (3, 1):
        tok_copies[j].start()
    w_copies = []
    for k in range(chunks):
        part = pl.ds(k * piece, piece)
        for p in range(2):
            w_copies.append(
                pltpu.make_async_copy(w_hbm.at[part, p, :], wv.at[p, part], w_sem.at[p, k])
            )

    col = lax.axis_index("col")
    ncol = topx.shape[0]
    side = lax.rem(col, 2)
    beside = col + 1 - 2 * side
    half = slots // 2
    barrier = pltpu.get_barrier_semaphore()
    for d in range(1, ncol):
        pl.semaphore_signal(
            barrier,
            inc=1,
            device_id={"col": lax.rem(col + d, ncol)},
            device_id_type=pl.DeviceIdType.MESH,
        )
    for j in (1, 2, 3):
        pl.semaphore_signal(
            barrier, inc=1, device_id={"row": where_to[j]}, device_id_type=pl.DeviceIdType.MESH
        )

    named = jnp.logical_or(routes_ref[0:1, :] == 0, routes_ref[1:2, :] == 0)
    flag = jnp.where(named, 1.0, 0.0)
    mask = jnp.broadcast_to(flag, (16, toks)).astype(jnp.bfloat16)
    before = lax.broadcasted_iota(jnp.int32, (toks, toks), 0)
    after = lax.broadcasted_iota(jnp.int32, (toks, toks), 1)
    ladder = jnp.where(before < after, 1.0, 0.0).astype(jnp.bfloat16)
    place = jnp.dot(mask, ladder, preferred_element_type=jnp.float32)[0:1, :].astype(jnp.int32)
    slot_id = lax.broadcasted_iota(jnp.int32, (slots, toks), 0)
    pick = jnp.where(slot_id == place, flag, 0.0).astype(jnp.bfloat16)
    half_id = lax.broadcasted_iota(jnp.int32, (half, toks), 0) + side * half
    half_pick = jnp.where(half_id == place, flag, 0.0).astype(jnp.bfloat16)
    pl.semaphore_wait(barrier, 3 + ncol - 1)

    pieces = y_send.shape[1]
    wide = rows // pieces

    def segment(j, k):
        lines = pl.ds(pl.multiple_of(j * slots + side * half, half), half)
        return sc_ref.at[lines, k * wide : (k + 1) * wide]

    far = []
    for n, j in enumerate((3, 1)):
        tok_copies[j].wait()
        if n == 1:
            for copy in (tok_copies[2], tok_copies[0], *w_copies):
                copy.start()
        hsend[n] = jnp.dot(half_pick, tokv[j], preferred_element_type=jnp.float32).astype(jnp.bfloat16)
        for k in range(pieces):
            block = hsend.at[n, :, k * wide : (k + 1) * wide]
            out = moved(block, segment(j, k), y_send.at[n, k], y_recv.at[n, k], where_to[j])
            out.start()
            on = moved(segment(j, k), segment(j, k), s_send.at[n, k], s_recv.at[n, k], beside, "col")
            far.append((out, on))
    tok_copies[2].wait()
    asend[...] = jnp.dot(pick, tokv[2], preferred_element_type=jnp.float32).astype(jnp.bfloat16)
    near = moved(asend, sc_ref.at[pl.ds(2 * slots, slots)], a_send, a_recv, partner)
    near.start()
    tok_copies[0].wait()
    sc_ref[0:slots, :] = jnp.dot(pick, tokv[0], preferred_element_type=jnp.float32).astype(jnp.bfloat16)

    folded[...] = jnp.zeros(folded.shape, jnp.float32)
    for k in range(chunks):
        for p in range(2):
            w_copies[2 * k + p].wait()

        def fold(t, carry, k=k):
            cols = pl.ds(pl.multiple_of(t * LANE, LANE), LANE)
            for p in range(2):
                tile = jnp.abs(wv[p, k * piece : (k + 1) * piece, cols])
                best = jnp.max(tile.reshape(-1, SUB, LANE), axis=0)
                folded[p, :, cols] = jnp.maximum(folded[p, :, cols], best)
            return carry

        lax.fori_loop(0, tiles, fold, 0)
        far[k][0].wait_recv()
        far[k][1].start()
    cmx[0] = jnp.zeros(cmx.shape[1:], jnp.float32)
    for p in range(2):
        cmx[0, p : p + 1, :] = jnp.max(folded[p], axis=0, keepdims=True)
    c_copies = []
    for j in (1, 2, 3):
        c_copies.append(moved(cmx.at[0], cmx.at[j], c_send.at[j - 1], c_recv.at[j - 1], where_to[j]))
        c_copies[-1].start()
    for out, on in far[chunks:]:
        out.wait_recv()
        on.start()
    for copy in c_copies:
        copy.wait()
    cm_ref[...] = jnp.maximum(jnp.maximum(cmx[0], cmx[1]), jnp.maximum(cmx[2], cmx[3]))
    near.wait()
    for out, on in far:
        out.wait_send()
        on.wait()
    tops[...] = jnp.zeros(tops.shape, jnp.float32)
    blocks = tops.shape[0] // 2

    def scale_row(t, p):
        cols = pl.ds(pl.multiple_of(t * LANE, LANE), LANE)
        return (cm_ref[p : p + 1, cols] + epsilon) / quant_range

    def swap(t):
        return moved(psend.at[t], prec.at[t], p_send.at[t], p_recv.at[t], partner)

    def cross(t):
        return moved(xsend.at[t], xrec.at[t], x_send.at[t], x_recv.at[t], across)

    def grad_block(t, j):
        return ga_ref.at[t, pl.ds(j * slots, slots)]

    def share_across(t):
        return moved(grad_block(t, 0), grad_block(t, 1), ga_send.at[t], ga_recv.at[t], across)

    def share_partner(t):
        return moved(grad_block(t, 0), grad_block(t, 2), gp_send.at[t], gp_recv.at[t], partner)

    def forward(t):
        return moved(grad_block(t, 1), grad_block(t, 3), gf_send.at[t], gf_recv.at[t], partner)

    def step(i, carry):
        @pl.when(i < tiles)
        def _():
            t = i
            halves = []
            for p in range(2):
                w = wv[p, :, pl.ds(pl.multiple_of(t * LANE, LANE), LANE)]
                halves.append((w * (1.0 / scale_row(t, p))).astype(jnp.bfloat16))
            quantized = jnp.concatenate(halves, axis=1)
            term = jnp.dot(sc_ref[...], quantized, preferred_element_type=jnp.float32)
            slot = lax.rem(t, 2)
            psend[t] = term[2 * slots :].astype(jnp.bfloat16)
            keep[slot] = term[: 2 * slots]
            swap(t).start()

        @pl.when(jnp.logical_and(i >= 1, i < tiles + 1))
        def _():
            t = i - 1
            slot = lax.rem(t, 2)
            swap(t).wait_recv()
            own[slot] = keep[slot, :slots] + prec[t, :slots].astype(jnp.float32)
            xsend[t] = (keep[slot, slots:] + prec[t, slots:].astype(jnp.float32)).astype(jnp.bfloat16)
            cross(t).start()

        @pl.when(jnp.logical_and(i >= 2, i < tiles + 2))
        def _():
            t = i - 2
            cross(t).wait_recv()
            total = own[lax.rem(t, 2)] + xrec[t].astype(jnp.float32)
            gate_pre = total[:, :LANE] * scale_row(t, 0)
            up_pre = total[:, LANE:] * scale_row(t, 1)
            gate_sig = jax.nn.sigmoid(gate_pre)
            gate_act = gate_pre * gate_sig
            cols = pl.ds(pl.multiple_of(t * LANE, LANE), LANE)
            hid_ref[:, cols] = (gate_act * up_pre).astype(jnp.bfloat16)
            upstream = dh_ref[:, cols].astype(jnp.float32)
            grad_gate = upstream * up_pre * gate_sig * (1.0 + gate_pre * (1.0 - gate_sig))
            grad_up = upstream * gate_act
            ga_ref[t, 0:slots, :] = jnp.concatenate([grad_gate, grad_up], axis=1).astype(jnp.bfloat16)
            share_across(t).start()
            share_partner(t).start()

        @pl.when(jnp.logical_and(i >= 3, i < tiles + 3))
        def _():
            t = i - 3
            share_across(t).wait_recv()
            forward(t).start()

        @pl.when(i < 4)
        def _():
            part = pl.ds(pl.multiple_of(i * (rows // 4), LANE), rows // 4)
            turned[part, :] = sc_ref[:, part].T

        @pl.when(i >= 4)
        def _():
            t = i - 4
            share_partner(t).wait_recv()
            forward(t).wait_recv()
            grad = jnp.dot(turned[...], ga_ref[t], preferred_element_type=jnp.float32)
            gbuf[t] = grad.astype(jnp.bfloat16)
            for b in range(blocks):
                for p in range(2):
                    tile = jnp.abs(grad[b * BLK : (b + 1) * BLK, p * LANE : (p + 1) * LANE])
                    best = jnp.max(tile.reshape(-1, SUB, LANE), axis=0)
                    tops[2 * b + p] = jnp.maximum(tops[2 * b + p], best)

        return carry

    lax.fori_loop(0, tiles + 4, step, 0)

    topx[0] = jnp.max(tops[...], axis=1)
    t_copies = []
    for d in range(1, ncol):
        t_copies.append(
            moved(topx.at[0], topx.at[d], t_send.at[d], t_recv.at[d], lax.rem(col + d, ncol), "col")
        )
        t_copies[-1].start()

    def finish(t, carry):
        swap(t).wait_send()
        cross(t).wait_send()
        share_across(t).wait_send()
        share_partner(t).wait_send()
        forward(t).wait_send()
        return carry

    lax.fori_loop(0, tiles, finish, 0)
    for copy in t_copies:
        copy.wait()
    top = topx[0]
    for d in range(1, ncol):
        top = jnp.maximum(top, topx[d])
    top_ref[...] = jnp.broadcast_to(jnp.max(top, axis=1, keepdims=True), top_ref.shape)


def update_kernel(inv_ref, cm_ref, wv, gv, update_hbm, new_hbm, uv, nv, u_sem, n_sem):
    blocks = u_sem.shape[1]
    tiles = gv.shape[0]

    def part(b):
        return pl.ds(pl.multiple_of(b * BLK, BLK), BLK)

    def put_update(b, p):
        return pltpu.make_async_copy(uv.at[p, part(b)], update_hbm.at[part(b), p, :], u_sem.at[p, b])

    def put_new(b, p):
        return pltpu.make_async_copy(nv.at[p, part(b)], new_hbm.at[part(b), p, :], n_sem.at[p, b])

    def step(b, carry):
        for p in range(2):
            inverse = inv_ref[2 * b + p]
            for t in range(tiles):
                cols = slice(t * LANE, (t + 1) * LANE)
                update = gv[t, part(b), p * LANE : (p + 1) * LANE].astype(jnp.float32) * inverse
                uv[p, part(b), cols] = update
                nv[p, part(b), cols] = wv[p, part(b), cols] - (learn_rate * cm_ref[p : p + 1, cols]) * update
            put_update(b, p).start()
            put_new(b, p).start()
        return carry

    def finish(b, carry):
        for p in range(2):
            put_update(b, p).wait()
            put_new(b, p).wait()
        return carry

    lax.fori_loop(0, blocks, step, 0)
    lax.fori_loop(0, blocks, finish, 0)


def on_device(tokens, routes, w_master, d_hidden):
    rows, _, columns = w_master.shape
    slots = d_hidden.shape[0]
    toks = tokens.shape[0]
    ncol = lax.axis_size("col")
    aligned = columns % LANE == 0 and rows % (4 * BLK) == 0 and slots % 32 == 0 and toks % LANE == 0
    if lax.axis_size("row") != 4 or ncol % 2 or not aligned:
        return on_device_plain(tokens, routes, w_master, d_hidden)
    tiles = columns // LANE
    bf16, f32 = jnp.bfloat16, jnp.float32
    chunks = 4
    pieces = 4
    blocks = rows // BLK
    vmem = pl.BlockSpec(memory_space=pltpu.VMEM)
    hbm = pl.BlockSpec(memory_space=pl.ANY)
    dma = pltpu.SemaphoreType.DMA
    wide = 2 * LANE
    hidden, grad, halves, colmax, tops = pl.pallas_call(
        forward_kernel,
        name="forward_exchange",
        out_shape=(
            jax.ShapeDtypeStruct((slots, columns), bf16),
            pltpu.VMEM((tiles, rows, wide), bf16),
            pltpu.VMEM((2, rows, columns), f32),
            jax.ShapeDtypeStruct((SUB, columns), f32),
            jax.ShapeDtypeStruct((2 * blocks, LANE), f32),
        ),
        in_specs=[vmem, vmem, hbm, hbm],
        out_specs=(vmem, vmem, vmem, vmem, vmem),
        scratch_shapes=[
            pltpu.VMEM((4 * slots, rows), bf16),
            pltpu.VMEM((tiles, 4 * slots, wide), bf16),
            pltpu.VMEM((rows, 4 * slots), bf16),
            pltpu.VMEM((2 * blocks, SUB, LANE), f32),
            pltpu.VMEM((ncol, 2 * blocks, LANE), f32),
            pltpu.VMEM((4, toks, rows), bf16),
            pltpu.VMEM((slots, rows), bf16),
            pltpu.VMEM((2, slots // 2, rows), bf16),
            pltpu.VMEM((2, SUB, columns), f32),
            pltpu.VMEM((4, SUB, columns), f32),
            pltpu.VMEM((tiles, 2 * slots, wide), bf16),
            pltpu.VMEM((tiles, 2 * slots, wide), bf16),
            pltpu.VMEM((2, 2 * slots, wide), f32),
            pltpu.VMEM((2, slots, wide), f32),
            pltpu.VMEM((tiles, slots, wide), bf16),
            pltpu.VMEM((tiles, slots, wide), bf16),
            dma((4,)),
            dma((2, chunks)),
            dma,
            dma,
            dma((2, pieces)),
            dma((2, pieces)),
            dma((2, pieces)),
            dma((2, pieces)),
            dma((ncol,)),
            dma((ncol,)),
            dma((3,)),
            dma((3,)),
        ]
        + [dma((tiles,))] * 10,
        compiler_params=pltpu.CompilerParams(
            collective_id=0, has_side_effects=True, vmem_limit_bytes=38 * 1024 * 1024
        ),
    )(routes.T, d_hidden, tokens, w_master)
    inverse = 1.0 / (tops[:, 0] + epsilon)
    update, new_master = pl.pallas_call(
        update_kernel,
        name="master_update",
        out_shape=(jax.ShapeDtypeStruct(w_master.shape, f32),) * 2,
        in_specs=[pl.BlockSpec(memory_space=pltpu.SMEM), vmem, vmem, vmem],
        out_specs=(hbm, hbm),
        scratch_shapes=[
            pltpu.VMEM((2, rows, columns), f32),
            pltpu.VMEM((2, rows, columns), f32),
            dma((2, blocks)),
            dma((2, blocks)),
        ],
        compiler_params=pltpu.CompilerParams(vmem_limit_bytes=30 * 1024 * 1024),
    )(
        inverse,
        colmax,
        pltpu.with_memory_space_constraint(halves, pltpu.VMEM),
        pltpu.with_memory_space_constraint(grad, pltpu.VMEM),
    )
    return (hidden, update, new_master)


def solution(mesh):
    in_specs = (P("row", None), P("row", None), P("row", None, "col"), P("row", "col"))
    out_specs = (P("row", "col"), P("row", None, "col"), P("row", None, "col"))
    return jax.shard_map(
        on_device, mesh=mesh, in_specs=in_specs, out_specs=out_specs, check_vma=False
    )
```
